32 devices in a mesh: section: 4 (over y, x), lon: 8 (over z, core).
Axes of the slice: x: 2, y: 2, z: 4, core: 2. Of those that a mesh axis runs over, the one named last changes fastest.
Arguments:
- fields: bfloat16 [4, 4, 6, 96, 192], P('section', None, None, 'lon'), may hold values from -6 to 6
- land_sea: int32 [6, 96], P(None, 'lon'), may hold values 0 or 1
- topography: int32 [6, 96], P(None, 'lon'), may hold values from 0 to 15
- land_embed: bfloat16 [2, 192], replicated, may hold values from -3 to 3
- topography_embed: bfloat16 [16, 192], replicated, may hold values from -3 to 3
- offsets: int32 [4], replicated, may hold values from 0 to 11, as said below
- norm_gain: bfloat16 [4, 2, 192], P('section'), may hold values from 0.5 to 1.5
- w_qkv: bfloat16 [4, 192, 576], P('section'), may hold values from -0.4375 to 0.4375
- w_out: bfloat16 [4, 192, 192], P('section'), may hold values from -0.4375 to 0.4375
- w_up: bfloat16 [4, 192, 768], P('section'), may hold values from -0.4375 to 0.4375
- w_down: bfloat16 [4, 768, 192], P('section'), may hold values from -0.21875 to 0.21875
- pos_bias: bfloat16 [4, 2, 6, 144, 144], P('section'), may hold values from -4 to 400
Outputs:
- forecast: bfloat16 [4, 4, 6, 96, 192], P('section', None, None, 'lon')
The draws below stay inside these ranges and needn't reach their ends.
Inputs may be any that keep to these rules, and one draw needn't show every extreme that they name: `offsets`: one entry equals 11.
All inputs are finite; a program needn't handle non-finite values. No bound on the sum of `land_sea` on one device may be relied on, other than what follows from the above.
Results may differ from the reference program's by a relative error of at most 0.023.
Values may be sent and summed in bfloat16 or wider, within the bound.
No kernel may reach another device: no remote copies, remote signals or barrier semaphores. Data moves between devices by JAX's collectives and lax.ppermute only.
A program may use at most 64 MiB of HBM per device.

```python
import jax
import jax.numpy as jnp
from jax import lax

C = 192
HEADS = 6
HD = 32
FFN = 768
WL = 2
WT = 6
WN = 12
HALF = 11
WTOK = 144
LEV = 4
LAT = 6
TYPES = 2
TOPO = 16
STEPS = 2
MICRO = 4
LON = 96
N_SECTION = 4


def draw_offsets(key, part):
    first_key, second_key = jax.random.split(key)
    drawn_offsets = jax.random.randint(first_key, (N_SECTION,), 0, HALF + 1)
    chosen_index = jax.random.randint(second_key, (), 0, N_SECTION)
    return jnp.where(jnp.arange(N_SECTION) == chosen_index, HALF, drawn_offsets).astype(jnp.int32)


def draw_pos_bias(key, part):
    bias_shape = (N_SECTION, TYPES, HEADS, WTOK, WTOK)
    subkeys = jax.random.split(key, 1)
    drawn = jnp.clip(jax.random.normal(subkeys[0], bias_shape, jnp.float32), -4.0, 4.0)
    return drawn.astype(jnp.bfloat16)


def plant(values, rng, low, top_value):
    dims = values.shape
    place = [jax.random.randint(jax.random.fold_in(rng, axis), (), 0, dims[axis]) for axis in range(len(dims))]
    values = values.at[tuple(place)].set(low)
    longest = dims.index(max(dims))
    place[longest] = (place[longest] + 1) % dims[longest]
    return values.at[tuple(place)].set(top_value)


def block_scale(key, extent, cuts, low, high):
    def one(axis_at, blocks):
        steps = jax.random.uniform(jax.random.fold_in(jax.random.fold_in(key, 6), axis_at), (blocks,), jnp.float32, low / len(cuts), high / len(cuts))
        return jnp.repeat(jnp.exp(steps), extent[axis_at] // blocks).reshape((-1,) + (1,) * (len(extent) - axis_at - 1))

    loudness = one(*cuts[0])
    for cut in cuts[1:]:
        loudness = loudness * one(*cut)
    return loudness


def noise(rng, dims, scale, most, cuts=(), dtype=jnp.bfloat16):
    factor_of = block_scale(rng, dims, cuts, -0.22, 0.18) if cuts else 1.0
    values = jax.random.normal(rng, dims, jnp.float32) * scale * factor_of
    return jnp.minimum(jnp.maximum(values, -most), most).astype(dtype)


def setup_inputs(seed: int = 0) -> dict:
    seeds = jax.random.split(jax.random.key(seed), 13)
    fields = noise(seeds[0], (MICRO, LEV, LAT, LON, C), 1.0, 6.0, ((0, 4), (3, 8)))
    land_sea = plant((jax.random.randint(seeds[1], (LAT, LON), 0, 10) < 3).astype(jnp.int32), jax.random.fold_in(seeds[1], 1), 0, 1)
    topography = plant(jax.random.randint(seeds[2], (LAT, LON), 0, TOPO), jax.random.fold_in(seeds[2], 1), 0, TOPO - 1).astype(jnp.int32)
    land_embed = noise(seeds[3], (2, C), 0.5, 3.0)
    topography_embed = noise(seeds[4], (TOPO, C), 0.5, 3.0)
    offsets = draw_offsets(jax.random.fold_in(seeds[12], 71), 0)
    norm_gain = jnp.clip(1.0 + 0.1 * jax.random.normal(seeds[6], (N_SECTION, 2, C), jnp.float32), 0.5, 1.5).astype(jnp.bfloat16)
    w_qkv = noise(seeds[7], (N_SECTION, C, 3 * C), C ** -0.5, 0.4375, ((0, 4),))
    w_out = noise(seeds[8], (N_SECTION, C, C), C ** -0.5, 0.4375, ((0, 4),))
    w_up = noise(seeds[9], (N_SECTION, C, FFN), C ** -0.5, 0.4375, ((0, 4),))
    w_down = noise(seeds[10], (N_SECTION, FFN, C), FFN ** -0.5, 0.21875, ((0, 4),))
    pos_bias = draw_pos_bias(jax.random.fold_in(seeds[12], 71), 0)
    return dict(fields=fields, land_sea=land_sea, topography=topography, land_embed=land_embed, topography_embed=topography_embed, offsets=offsets, norm_gain=norm_gain, w_qkv=w_qkv, w_out=w_out, w_up=w_up, w_down=w_down, pos_bias=pos_bias)


def layer_norm(stream, gain):
    average = lax.optimization_barrier(jnp.mean(stream, axis=-1, keepdims=True))
    centred = stream - average
    variance = lax.optimization_barrier(jnp.mean(centred * centred, axis=-1, keepdims=True))
    return (centred * lax.rsqrt(variance + 1e-05) * gain.astype(jnp.float32)).astype(jnp.bfloat16)

def to_windows(tokens):
    level_count, lat_count, lon_count, feature = tokens.shape
    tokens = tokens.reshape(level_count // WL, WL, lat_count // WT, WT, lon_count // WN, WN, feature)
    tokens = tokens.transpose(0, 2, 4, 1, 3, 5, 6)
    return tokens.reshape(level_count // WL * (lat_count // WT), lon_count // WN, WL * WT * WN, feature)

def from_windows(tokens, level_count, lat_count, lon_count):
    feature = tokens.shape[-1]
    tokens = tokens.reshape(level_count // WL, lat_count // WT, lon_count // WN, WL, WT, WN, feature)
    tokens = tokens.transpose(0, 3, 1, 4, 2, 5, 6)
    return tokens.reshape(level_count, lat_count, lon_count, feature)

def window_attention(normed, w_qkv, pos_bias):
    level_count, lat_count, lon_count, feature = normed.shape
    tokens_win = to_windows(normed)
    qkv = jnp.einsum('ynwc,cd->ynwd', tokens_win.astype(jnp.float32), w_qkv.astype(jnp.float32)).astype(jnp.bfloat16)
    type_count, window_count, window_len, _ = qkv.shape
    qkv = qkv.reshape(type_count, window_count, window_len, 3, HEADS, HD)
    query_heads = qkv[:, :, :, 0].astype(jnp.float32)
    key_heads = qkv[:, :, :, 1].astype(jnp.float32)
    value_heads = qkv[:, :, :, 2].astype(jnp.float32)
    scores = jnp.einsum('ynqhd,ynkhd->ynhqk', query_heads, key_heads) * HD ** (-0.5)
    scores = scores + pos_bias.astype(jnp.float32)[:, None]
    attn_probs = jax.nn.softmax(scores, axis=-1).astype(jnp.bfloat16)
    mixed_heads = jnp.einsum('ynhqk,ynkhd->ynqhd', attn_probs.astype(jnp.float32), value_heads).astype(jnp.bfloat16)
    mixed_heads = mixed_heads.reshape(type_count, window_count, window_len, feature)
    return from_windows(mixed_heads, level_count, lat_count, lon_count)

def reference(fields, land_sea, topography, land_embed, topography_embed, offsets, norm_gain, w_qkv, w_out, w_up, w_down, pos_bias):
    surface = land_embed.astype(jnp.float32)[land_sea] + topography_embed.astype(jnp.float32)[topography]

    def one_block(current, block_index):
        shift = offsets[block_index]
        stream = current.astype(jnp.float32)
        normed = layer_norm(stream, norm_gain[block_index, 0])
        rolled = jnp.roll(normed, -shift, axis=2)
        heads_out = window_attention(rolled, w_qkv[block_index], pos_bias[block_index])
        mixed_back = jnp.roll(heads_out, shift, axis=2)
        attn_proj = jnp.einsum('ltnc,cd->ltnd', mixed_back.astype(jnp.float32), w_out[block_index].astype(jnp.float32))
        after_attn = (stream + attn_proj).astype(jnp.bfloat16)
        after_stream = after_attn.astype(jnp.float32)
        normed2 = layer_norm(after_stream, norm_gain[block_index, 1])
        up_proj = jnp.einsum('ltnc,cf->ltnf', normed2.astype(jnp.float32), w_up[block_index].astype(jnp.float32))
        activated = jax.nn.gelu(up_proj, approximate=False).astype(jnp.bfloat16)
        down_proj = jnp.einsum('ltnf,fc->ltnc', activated.astype(jnp.float32), w_down[block_index].astype(jnp.float32))
        return (after_stream + down_proj).astype(jnp.bfloat16)

    def rollout(sample):
        current = sample
        for repeat in range(STEPS):
            current = (current.astype(jnp.float32) + surface).astype(jnp.bfloat16)
            for block_index in range(N_SECTION):
                current = one_block(current, block_index)
        return current
    return lax.map(rollout, fields)
```

```python
import functools

import jax
import jax.numpy as jnp
from jax import lax
from jax.experimental import pallas as pl
from jax.experimental.pallas import tpu as pltpu
from jax.sharding import PartitionSpec as P

F32 = jnp.float32
BF = jnp.bfloat16
LANE = 128
VMEM_LIMIT = 8 << 20
HEADS = 6
HD = 32
WL = 2
WT = 6
WN = 12
STEPS = 2
WTOK = WL * WT * WN
C = HEADS * HD
PAD = 2 * LANE
TAIL = WTOK - LANE
NT = (((1,), (1,)), ((), ()))
VM = pl.BlockSpec(memory_space=pltpu.VMEM)
SM = pl.BlockSpec(memory_space=pltpu.SMEM)
ANY = pl.BlockSpec(memory_space=pl.ANY)


def call(kernel, name, in_specs, out_shape, scratch=()):
    many = isinstance(out_shape, (list, tuple))
    return pl.pallas_call(
        kernel,
        out_shape=out_shape,
        in_specs=in_specs,
        out_specs=[VM] * len(out_shape) if many else VM,
        scratch_shapes=list(scratch),
        name=name,
        compiler_params=pltpu.CompilerParams(vmem_limit_bytes=VMEM_LIMIT),
    )


def dot(a, b):
    return jnp.dot(a, b, preferred_element_type=F32)


def iota(shape, dim):
    return lax.broadcasted_iota(jnp.int32, shape, dim)


def shift_matrix(delta, base):
    row, col = iota((WTOK, 2 * WTOK), 0), iota((WTOK, 2 * WTOK), 1)
    n = row - WN * ((row * 43691) >> 19)
    src = row + delta + jnp.where(n + delta < WN, base, WTOK - WN - base)
    return jnp.where(col == src, 1.0, 0.0).astype(BF)


def norm(x, gain):
    mean = jnp.sum(x, axis=-1, keepdims=True) * (1.0 / C)
    cen = x - mean
    var = jnp.sum(cen * cen, axis=-1, keepdims=True) * (1.0 / C)
    return (cen * lax.rsqrt(var + 1e-5) * gain).astype(BF)


def gelu(v):
    return 0.5 * v * (1.0 + lax.erf(v * (2.0**-0.5)))


def spread(t):
    lane = iota((WTOK, C), 1)
    zero = jnp.zeros((), BF)
    parts = [jnp.where((lane >= h * HD) & (lane < (h + 1) * HD), t, zero) for h in range(HEADS)]
    rest = jnp.zeros((LANE - HEADS * TAIL, C), BF)
    return jnp.concatenate([p[:LANE] for p in parts] + [p[LANE:] for p in parts] + [rest], axis=0)


def attention(q, k, v, bias_ref):
    s = lax.dot_general(q, spread(k), NT, preferred_element_type=F32)
    scale = HD**-0.5
    tiles = []
    for h in range(HEADS + 1):
        cols = slice(LANE * h, LANE * (h + 1))
        tiles.append(s[:, cols] * scale + bias_ref[:, cols].astype(F32))
    lane = iota((WTOK, LANE), 1)
    tail = tiles[HEADS]
    low = jnp.float32(-1e30)
    probs = []
    tail_top = jnp.zeros((WTOK, LANE), F32)
    for h in range(HEADS):
        mine = (lane >= TAIL * h) & (lane < TAIL * (h + 1))
        top = jnp.max(jnp.maximum(tiles[h], jnp.where(mine, tail, low)), axis=-1, keepdims=True)
        tail_top = jnp.where(mine, top, tail_top)
        probs.append(jnp.exp(tiles[h] - top).astype(BF))
    used = lane < TAIL * HEADS
    probs.append(jnp.where(used, jnp.exp(jnp.where(used, tail - tail_top, 0.0)), 0.0).astype(BF))
    p = jnp.concatenate(probs, axis=1)
    total = dot(p, spread(jnp.ones((WTOK, C), BF)))
    return (dot(p, spread(v)) / total).astype(BF)


def block_kernel(first, d_ref, a_ref, b_ref, wp_ref, up_ref, down_ref, bias_ref, gain_ref, emb_ref, o_ref):
    both = jnp.concatenate([a_ref[...], b_ref[...]], axis=0)
    state = dot(shift_matrix(d_ref[0], 0), both)
    x = state[:, :C]
    if first:
        x = x + dot(state[:, LANE:].astype(BF), emb_ref[...])
        x = x.astype(BF).astype(F32)
    gain = gain_ref[...].astype(F32)
    n = norm(x, gain[0:1])
    q, k, v = (dot(n, wp_ref[:, PAD * p : PAD * p + C]).astype(BF) for p in range(3))
    mixed = attention(q, k, v, bias_ref)
    y = (x + dot(mixed, wp_ref[:, 3 * PAD : 3 * PAD + C])).astype(BF).astype(F32)
    n2 = norm(y, gain[1:2])
    act = gelu(dot(n2, up_ref[...])).astype(BF)
    o_ref[:, :C] = (y + dot(act, down_ref[...])).astype(BF)
    o_ref[:, C:] = state[:, C:].astype(BF)


def block(first, delta, a, b, weights):
    return call(
        functools.partial(block_kernel, first),
        "block_first" if first else "block",
        [SM] + [VM] * 8,
        jax.ShapeDtypeStruct((WTOK, PAD), BF),
    )(delta, a, b, *weights)


def pack_kernel(i_ref, qkv_ref, out_ref, up_ref, down_ref, gain_ref, bias_ref, a_ref, b_ref, as_ref, bs_ref):
    kind, core = i_ref[0], i_ref[1]
    a_ref[0, :, : 3 * C] = qkv_ref[...]
    a_ref[0, :, 3 * C :] = out_ref[...]
    bias = [bias_ref[kind, h] for h in range(HEADS)]
    for h in range(HEADS):
        a_ref[1, :WTOK, LANE * h : LANE * (h + 1)] = bias[h][:, :LANE]
    a_ref[1, WTOK:, :] = jnp.zeros((C - WTOK, 4 * C), BF)
    tail = jnp.concatenate([b[:, LANE:] for b in bias] + [jnp.zeros((WTOK, LANE - HEADS * TAIL), BF)], axis=1)
    rows = WTOK // HEADS
    for j in range(HEADS):
        a_ref[1, WTOK : WTOK + rows, LANE * j : LANE * (j + 1)] = tail[rows * j : rows * (j + 1)]
    a_ref[1, WTOK + rows : WTOK + rows + 2, :C] = gain_ref[...]
    b_ref[0] = up_ref[...]
    for j in range(4):
        b_ref[1, :, C * j : C * (j + 1)] = down_ref[C * j : C * (j + 1)]
    as_ref[...] = a_ref[core]
    bs_ref[...] = b_ref[core]


def collect_kernel(sources, i_ref, own_a, own_b, *refs):
    cands, outs = refs[: 4 * (sources - 1)], refs[4 * (sources - 1) :]
    wp_ref, up_ref, down_ref, bias_ref, gain_ref, ab, sem = outs
    pick, core = i_ref[0], i_ref[1]

    def fetch(src, slot):
        return pltpu.make_async_copy(src, ab.at[slot], sem)

    @pl.when(pick == 0)
    def _():
        copies = [fetch(own_a.at[0], 0), fetch(own_a.at[1], 1), fetch(own_b.at[0], 2), fetch(own_b.at[1], 3)]
        for c in copies:
            c.start()
        for c in copies:
            c.wait()

    for k in range(1, sources):
        mine_a, mine_b, other_a, other_b = cands[4 * (k - 1) : 4 * k]

        @pl.when(pick == k)
        def _():
            copies = [
                fetch(mine_a, core),
                fetch(other_a, 1 - core),
                fetch(mine_b, 2 + core),
                fetch(other_b, 3 - core),
            ]
            for c in copies:
                c.start()
            for c in copies:
                c.wait()

    for p in range(4):
        wp_ref[:, PAD * p : PAD * p + C] = ab[0, :, C * p : C * (p + 1)]
        down_ref[C * p : C * (p + 1), :] = ab[3, :, C * p : C * (p + 1)]
    up_ref[...] = ab[2]
    bias_ref[:, : HEADS * LANE] = ab[1, :WTOK, :]
    rows = WTOK // HEADS
    for j in range(HEADS):
        bias_ref[rows * j : rows * (j + 1), HEADS * LANE :] = ab[1, WTOK : WTOK + rows, LANE * j : LANE * (j + 1)]
    gain_ref[...] = ab[1, WTOK + rows : WTOK + rows + 2, :C]


def merge_kernel(i_ref, w1_ref, w2_ref, w3_ref, w4_ref, o_ref):
    delta, parity = i_ref[0], i_ref[1]
    for n, (lo, hi) in enumerate(((w4_ref, w1_ref), (w3_ref, w2_ref))):
        both = jnp.concatenate([lo[:, :C], hi[:, :C]], axis=0)
        picked = dot(shift_matrix(delta, WTOK * parity), both).astype(BF)
        o_ref[(n + parity) % 2] = picked


def solution(mesh):
    sections, strips = mesh.shape["section"], mesh.shape["lon"]
    kinds = 2
    ring = strips // kinds
    order = [*range(0, ring, 2), *reversed(range(1, ring, 2))]
    place = [[ring * kind + r for r in order] for kind in range(kinds)]

    def on_device(fields, land_sea, topography, land_embed, topography_embed, offsets, gains, w_qkv, w_out, w_up, w_down, bias):
        sec, lon = lax.axis_index("section"), lax.axis_index("lon")
        kind, core = lon // ring, lon % 2
        classes = land_embed.shape[0] + topography_embed.shape[0]
        spare = PAD - C

        ints = jnp.stack([kind, core]).astype(jnp.int32)
        half = jax.ShapeDtypeStruct((C, 4 * C), BF)
        full = jax.ShapeDtypeStruct((2, C, 4 * C), BF)
        own_a, own_b, send_a, send_b = call(pack_kernel, "pack", [SM] + [VM] * 6, [full, full, half, half])(
            ints, w_qkv[0], w_out[0], w_up[0], w_down[0], gains[0], bias[0]
        )
        partner = [(i, i ^ 1) for i in range(strips)]
        cands = []
        for k in range(1, sections):
            perm = [(i, i ^ k) for i in range(sections)]
            mine_a = lax.ppermute(send_a, "section", perm)
            mine_b = lax.ppermute(send_b, "section", perm)
            other_a = lax.ppermute(mine_a, "lon", partner)
            other_b = lax.ppermute(mine_b, "lon", partner)
            cands += [mine_a, mine_b, other_a, other_b]

        def weights_of(b):
            pick = jnp.stack([sec ^ b, core]).astype(jnp.int32)
            return call(
                functools.partial(collect_kernel, sections),
                "collect",
                [SM] + [ANY] * (2 + len(cands)),
                [
                    jax.ShapeDtypeStruct((C, 4 * PAD), BF),
                    jax.ShapeDtypeStruct((C, 4 * C), BF),
                    jax.ShapeDtypeStruct((4 * C, C), BF),
                    jax.ShapeDtypeStruct((WTOK, LANE * (HEADS + 1)), BF),
                    jax.ShapeDtypeStruct((2, C), BF),
                ],
                [pltpu.VMEM((4, C, 4 * C), BF), pltpu.SemaphoreType.DMA],
            )(pick, own_a, own_b, *cands)

        table = jnp.concatenate([land_embed, topography_embed], axis=0)
        table = jnp.pad(table, ((LANE - spare, spare - classes), (0, 0)))

        cls = jnp.arange(spare, dtype=jnp.int32)
        hot = (land_sea[..., None] == cls) | (topography[..., None] + land_embed.shape[0] == cls)
        hot = jnp.broadcast_to(hot.astype(BF)[None], (WL, WT, WN, spare)).reshape(WTOK, spare)
        levels = fields.reshape(kinds, WTOK, C)
        got = []
        for turn in range(2):
            piece = lax.dynamic_index_in_dim(levels, (core + turn) % 2, 0, keepdims=False)
            piece = jnp.concatenate([piece, hot], axis=1)
            perm = [(j, place[(j + turn) % 2][j // 2]) for j in range(strips)]
            got.append(lax.ppermute(piece, "lon", perm))
        w0 = jnp.where(kind == 0, got[0], got[1])
        w1 = jnp.where(kind == 0, got[1], got[0])

        west = [(place[kd][(r + 1) % ring], place[kd][r]) for kd in range(kinds) for r in range(ring)]
        ready = [[*weights_of(b), table] for b in range(sections)]
        frame = jnp.int32(0)
        for t in range(STEPS * sections):
            b = t % sections
            delta = (offsets[b] - frame) % WN
            frame = frame + delta
            d = delta.reshape(1)
            edge = lax.ppermute(w0, "lon", west)
            n0 = block(b == 0, d, w0, w1, ready[b])
            n1 = block(b == 0, d, w1, edge, ready[b])
            w0, w1 = n0, n1

        def send_home(turn):
            def go(w0, w1):
                out = []
                for slot, w in enumerate((w0, w1)):
                    for role in range(2):
                        perm = []
                        for kd in range(kinds):
                            for r in range(ring):
                                home = 2 * r + slot + turn + (kd ^ role)
                                perm.append((place[kd][r], home % strips))
                        out.append(lax.ppermute(w, "lon", perm))
                return tuple(out)

            return go

        turn = (frame // WN) % strips
        homes = lax.switch(turn, [send_home(q) for q in range(strips)], w0, w1)
        parity = (lon - turn) % 2
        ints = jnp.stack([WN - frame % WN, parity]).astype(jnp.int32)
        out = call(merge_kernel, "merge", [SM] + [VM] * 4, jax.ShapeDtypeStruct((kinds, WTOK, C), BF))(ints, *homes)
        return out.reshape(fields.shape)

    return jax.shard_map(
        on_device,
        mesh=mesh,
        in_specs=(
            P("section", None, None, "lon", None),
            P(None, "lon"),
            P(None, "lon"),
            P(),
            P(),
            P(),
            P("section", None, None),
            P("section", None, None),
            P("section", None, None),
            P("section", None, None),
            P("section", None, None),
            P("section", None, None, None, None),
        ),
        out_specs=P("section", None, None, "lon", None),
        check_vma=False,
    )
```
